32 devices in a mesh: src: 16 (over z, y, core), tgt: 2 (over x).
Axes of the slice: x: 2, y: 2, z: 4, core: 2. Of those that a mesh axis runs over, the one named last changes fastest.
Arguments:
- source_mean: float32 [16, 4096], P(None, 'src'), may hold values from -1 to 1, as said below
- target_points: float32 [16, 8192], P(None, 'tgt'), may hold values from -1 to 1
- precision: float32 [16], replicated, may hold values from 0.25 to 2, as said below
- target_values: float32 [8192, 128], P('tgt'), may hold values from 0.5 to 3
- cash: float32 [4096, 128], P('src'), may hold values from -3 to 3
- salvage: float32 [4096, 128], P('src'), may hold values from 0.5 to 3
- switch_cost: float32 [128], replicated, may hold values from 0.05 to 0.5
- cotangent: float32 [4096, 128], P('src'), may hold values from -0.5 to 1.5
- decision: int32 [4096, 128], P('src'), may hold values from 0 to 2
Outputs:
- source_value: float32 [4096, 128], P('src')
- target_adjoint: float32 [2, 4096, 128], P('tgt', 'src')
The draws below stay inside these ranges and needn't reach their ends.
Inputs may be any that keep to these rules, and one draw needn't show every extreme that they name: `source_mean`: the first factor of source i lies between -1 + 2 i / 4096 and -1 + 2 (i + 1) / 4096. The first factor's precision is 1.5 or more.
All inputs are finite; a program needn't handle non-finite values.
Results may differ from the reference program's by a relative error of at most 0.00024.
Values sent between devices are 32-bit elements; how exact they have to be, the bound alone decides.
No kernel may reach another device: no remote copies, remote signals or barrier semaphores. Data moves between devices by JAX's collectives and lax.ppermute only.
A program may use at most 64 MiB of HBM per device.

```python
import math
import jax
import jax.numpy as jnp
from jax import lax

F = 16
M = 128
SRC_DEV = 256
TGT_DEV = 4096
NS = 4096
NT = 8192
N_SRC = 16


def draw_source_mean(key, part):
    first_key, second_key = jax.random.split(key)
    jitter = jax.random.uniform(first_key, (NS,), jnp.float32)
    leading = -1.0 + 2.0 * (jnp.arange(NS, dtype=jnp.float32) + jitter) / NS
    leading = jnp.clip(leading, -1.0, 1.0)
    others = jax.random.uniform(second_key, (F - 1, NS), jnp.float32, minval=-1.0, maxval=1.0)
    return jnp.concatenate([leading[None, :], others], axis=0)


def draw_precision(key, part):
    first_key, second_key = jax.random.split(key)
    leading = jax.random.uniform(first_key, (1,), jnp.float32, minval=1.5, maxval=2.0)
    others = jnp.exp(jax.random.uniform(second_key, (F - 1,), jnp.float32, minval=math.log(0.25), maxval=math.log(2.0)))
    return jnp.concatenate([leading, others], axis=0)


def plant(drawn, rng, smallest, top_value):
    dims = drawn.shape
    place = [jax.random.randint(jax.random.fold_in(rng, axis), (), 0, dims[axis]) for axis in range(len(dims))]
    drawn = drawn.at[tuple(place)].set(smallest)
    longest = dims.index(max(dims))
    place[longest] = (place[longest] + 1) % dims[longest]
    return drawn.at[tuple(place)].set(top_value)


def shard_levels(stream_key, shape, cuts, smallest, top_value):
    level, own = 1.0, jax.random.fold_in(stream_key, 6)
    for dim, parts in cuts:
        steps = jnp.exp(jax.random.uniform(jax.random.fold_in(own, dim), (parts,), jnp.float32, smallest / len(cuts), top_value / len(cuts)))
        level = level * jnp.repeat(steps, shape[dim] // parts).reshape([-1 if axis == dim else 1 for axis in range(len(shape))])
    return level


def noise(key, shape, deviation, limit, cuts=(), kind=jnp.bfloat16):
    gain = shard_levels(key, shape, cuts, -0.22, 0.18) if cuts else 1.0
    drawn = jax.random.normal(key, shape, jnp.float32) * deviation * gain
    return jnp.minimum(jnp.maximum(drawn, -limit), limit).astype(kind)


def setup_inputs(seed: int = 0) -> dict:
    keys = jax.random.split(jax.random.key(seed), 10)
    return {
        "source_mean": draw_source_mean(jax.random.fold_in(keys[9], 71), 0),
        "target_points": jnp.clip(jax.random.uniform(keys[1], (F, NT), jnp.float32, -1.0, 1.0) * shard_levels(keys[1], (F, NT), ((1, 2),), -0.4, 0.0), -1.0, 1.0),
        "precision": draw_precision(jax.random.fold_in(keys[9], 71), 0),
        "target_values": jnp.clip(0.5 + 2.5 * jax.random.uniform(keys[3], (NT, M), jnp.float32) ** shard_levels(keys[3], (NT, M), ((0, 2),), -0.2, 0.2), 0.5, 3.0),
        "cash": noise(keys[4], (NS, M), 0.5, 3.0, ((0, 16),), jnp.float32),
        "salvage": jnp.clip(0.5 + 2.5 * jax.random.uniform(keys[5], (NS, M), jnp.float32) ** shard_levels(keys[5], (NS, M), ((0, 16),), -0.2, 0.2), 0.5, 3.0),
        "switch_cost": jnp.clip(jnp.exp(jax.random.uniform(keys[6], (M,), jnp.float32, math.log(0.05), math.log(0.5))), 0.05, 0.5),
        "cotangent": jnp.clip(-0.5 + 2.0 * jax.random.uniform(keys[7], (NS, M), jnp.float32) ** shard_levels(keys[7], (NS, M), ((0, 16),), -0.2, 0.2), -0.5, 1.5),
        "decision": plant(jax.random.randint(keys[8], (NS, M), 0, 3), jax.random.fold_in(keys[8], 1), 0, 2).astype(jnp.int32),
    }


def choose_value(continuation, cash_part, salvage_part, cost_part):
    hold_value = continuation + cash_part
    paired = hold_value.reshape(hold_value.shape[0], -1, 2)[:, :, ::-1].reshape(hold_value.shape)
    switched = paired - cost_part[None, :]
    return jnp.maximum(jnp.maximum(hold_value, switched), salvage_part)


def adjoint_input(cotangent, decision):
    held = jnp.where(decision == 0, cotangent, 0.0)
    moved = jnp.where(decision == 1, cotangent, 0.0)
    swapped = moved.reshape(moved.shape[0], -1, 2)[:, :, ::-1].reshape(moved.shape)
    return held + swapped


def block_density(scaled_part, offset_part, target_points):
    cross = lax.dot_general(scaled_part, target_points, (((0,), (0,)), ((), ())), precision=lax.Precision.HIGHEST, preferred_element_type=jnp.float32)
    return jnp.exp(cross + offset_part[:, None])


def reference(source_mean, target_points, precision, target_values, cash, salvage, switch_cost, cotangent, decision):
    scaled = source_mean * precision[:, None]
    offset = -0.5 * jnp.sum(scaled * source_mean, axis=0)
    scaled_blocks = scaled.reshape(F, N_SRC, SRC_DEV).transpose(1, 0, 2)
    offset_blocks = offset.reshape(N_SRC, SRC_DEV)
    adjoint_in = adjoint_input(cotangent, decision)
    adjoint_blocks = adjoint_in.reshape(N_SRC, SRC_DEV, M)

    def add_columns(running, pieces):
        dens_block = block_density(pieces[0], pieces[1], target_points)
        return running + jnp.sum(dens_block, axis=0), None

    column_sum, _ = lax.scan(add_columns, jnp.zeros((NT,), jnp.float32), (scaled_blocks, offset_blocks))
    factor = (NS / NT) / column_sum
    scaled_values = target_values * factor[:, None]

    def both_products(running, pieces):
        dens_block = block_density(pieces[0], pieces[1], target_points)
        cont_block = jnp.dot(dens_block, scaled_values, precision=lax.Precision.HIGHEST, preferred_element_type=jnp.float32)
        back_part = lax.dot_general(dens_block, pieces[2], (((0,), (0,)), ((), ())), precision=lax.Precision.HIGHEST, preferred_element_type=jnp.float32)
        return running + back_part, cont_block

    raw_sum, cont_blocks = lax.scan(both_products, jnp.zeros((NT, M), jnp.float32), (scaled_blocks, offset_blocks, adjoint_blocks))
    continuation = cont_blocks.reshape(NS, M)
    source_value = choose_value(continuation, cash, salvage, switch_cost)
    target_adjoint = (raw_sum * factor[:, None]).reshape(NT // TGT_DEV, TGT_DEV, M)
    return source_value, target_adjoint
```

```python
import math

import jax
import jax.numpy as jnp
from jax import lax
from jax.experimental import pallas as pl
from jax.experimental.pallas import tpu as pltpu
from jax.sharding import PartitionSpec as P

LOG2E = math.log2(math.e)
F32 = jnp.float32
BF16 = jnp.bfloat16


def split2(x):
    hi = x.astype(BF16)
    return hi, (x - hi.astype(F32)).astype(BF16)


def split3(x):
    hi = x.astype(BF16)
    rest = x - hi.astype(F32)
    mid = rest.astype(BF16)
    return hi, mid, (rest - mid.astype(F32)).astype(BF16)


def dot(left, right, left_dim, right_dim):
    return lax.dot_general(left, right, (((left_dim,), (right_dim,)), ((), ())), preferred_element_type=F32)


def source_terms(mean, scale):
    scaled = mean * (scale * LOG2E)
    offset = -0.5 * jnp.sum(scaled * mean, axis=0, keepdims=True)
    s1, s2, s3 = split3(scaled)
    row = lax.broadcasted_iota(jnp.int32, scaled.shape, 0)
    o1, o2, o3 = (jnp.broadcast_to(o.astype(F32), scaled.shape) for o in split3(offset))
    tail = jnp.where(row == 0, o1, jnp.where(row == 1, o2, jnp.where(row == 2, o3, 0.0))).astype(BF16)
    return jnp.concatenate([s1, s1, s2, s2, s1, s3, tail], axis=0)


def target_terms(points):
    t1, t2, t3 = split3(points)
    row = lax.broadcasted_iota(jnp.int32, points.shape, 0)
    tail = jnp.where(row < 3, 1.0, 0.0).astype(BF16)
    return jnp.concatenate([t1, t2, t1, t2, t3, t1, tail], axis=0)


def swap_pairs(x):
    lane = lax.broadcasted_iota(jnp.int32, x.shape, 1)
    width = x.shape[1]
    return jnp.where(lane % 2 == 0, pltpu.roll(x, width - 1, 1), pltpu.roll(x, 1, 1))


def pack_kernel(mean, cotangent, decision, out):
    rows, lanes = cotangent.shape
    held = jnp.where(decision[...] == 0, cotangent[...], 0.0)
    moved = jnp.where(decision[...] == 1, cotangent[...], 0.0)
    out[0:rows, :] = held + swap_pairs(moved)
    factors = mean.shape[0]
    for part in range(mean.shape[1] // lanes):
        out[rows + part * factors : rows + (part + 1) * factors, :] = mean[:, part * lanes : (part + 1) * lanes]


def density_kernel(mean, scale, points, density, column_sum):
    left = source_terms(mean[...], scale[...])
    width = 256
    for j in range(points.shape[1] // width):
        cols = slice(j * width, (j + 1) * width)
        tile = jnp.exp2(dot(left, target_terms(points[:, cols]), 0, 0))
        density[:, cols] = tile
        column_sum[:, cols] = jnp.sum(tile, axis=0, keepdims=True)


def continuation_kernel(density, total, values, out, *, ratio):
    width = 256
    lanes = values.shape[1]
    acc = jnp.zeros((density.shape[0], 2 * lanes), F32)
    low = jnp.zeros((density.shape[0], lanes), F32)
    for j in range(density.shape[1] // width):
        cols = slice(j * width, (j + 1) * width)
        factor = ratio / total[:, cols]
        hi, lo = split2(density[:, cols] * factor)
        vhi, vlo = split2(values[cols, :])
        acc += dot(hi, jnp.concatenate([vhi, vlo], axis=1), 1, 0)
        low += dot(lo, vhi, 1, 0)
    out[...] = acc[:, :lanes] + (acc[:, lanes:] + low)


def adjoint_kernel(scale, points, *refs):
    blocks, out = refs[:-1], refs[-1]
    lanes = out.shape[1]
    factors = points.shape[0]
    rows = out.shape[0]
    step = min(256, rows)
    rights, pairs = [], []
    for block in blocks:
        body = block.shape[0] * lanes // (lanes + factors)
        mean = jnp.concatenate(
            [block[body + p * factors : body + (p + 1) * factors, :] for p in range(body // lanes)], axis=1
        )
        rights.append(source_terms(mean, scale[...]))
        ahi, alo = split2(block[0:body, :])
        pairs.append((jnp.concatenate([ahi, alo], axis=1), ahi))
    for t in range(rows // step):
        left = target_terms(points[:, t * step : (t + 1) * step])
        acc = jnp.zeros((step, 2 * lanes), F32)
        low = jnp.zeros((step, lanes), F32)
        for right, (both, ahi) in zip(rights, pairs):
            hi, lo = split2(jnp.exp2(dot(left, right, 0, 0)))
            acc += dot(hi, both, 1, 0)
            low += dot(lo, ahi, 1, 0)
        out[t * step : (t + 1) * step, :] = acc[:, :lanes] + (acc[:, lanes:] + low)


def value_kernel(own, other, cash, salvage, cost, out):
    hold = own[...] + other[...] + cash[...]
    out[...] = jnp.maximum(jnp.maximum(hold, swap_pairs(hold) - cost[...]), salvage[...])


def call(kernel, out_shape, *args, name):
    return pl.pallas_call(kernel, out_shape=out_shape, name=name)(*args)


def shape(*dims):
    return jax.ShapeDtypeStruct(dims, F32)


def on_device(source_mean, target_points, precision, target_values, cash, salvage, switch_cost, cotangent, decision):
    n = lax.axis_size("src")
    nt = lax.axis_size("tgt")
    factors, sources = source_mean.shape
    targets = target_points.shape[1]
    lanes = cash.shape[1]
    me = lax.axis_index("src")
    scale = precision[:, None]
    ratio = (sources * n) / (targets * nt)
    rows = targets // n
    group = 4

    def flip(x, mask):
        return lax.ppermute(x, "src", [(i, i ^ mask) for i in range(n)])

    packed = call(pack_kernel, shape(sources + factors * sources // lanes, lanes), source_mean, cotangent, decision, name="pack")
    blocks = [packed]
    bit = group
    while bit < n:
        span = min(4, n // bit)
        payload = blocks[0] if len(blocks) == 1 else jnp.stack(blocks)
        received = [flip(payload, k * bit) for k in range(1, span)]
        more = []
        for r in received:
            more += [r] if len(blocks) == 1 else [r[b] for b in range(len(blocks))]
        blocks = blocks + more
        bit *= span

    density, total = call(density_kernel, (shape(sources, targets), shape(1, targets)), source_mean, scale, target_points, name="density")
    mask = 1
    while mask < n:
        total = total + flip(total, mask)
        mask *= 2

    start = (me // group) * (group * rows)
    near_points = lax.dynamic_slice(target_points, (0, start), (factors, group * rows))
    part = call(adjoint_kernel, shape(group * rows, lanes), scale, near_points, *blocks, name="adjoint")
    part = part.reshape(2, 2, rows, lanes)
    core, far = me % 2, (me // 2) % 2
    keep = lax.dynamic_index_in_dim(part, core, 1, keepdims=False)
    send = lax.dynamic_index_in_dim(part, 1 - core, 1, keepdims=False)
    half = keep + flip(send, 1)
    keep = lax.dynamic_index_in_dim(half, far, 0, keepdims=False)
    send = lax.dynamic_index_in_dim(half, 1 - far, 0, keepdims=False)
    own_sum = keep + flip(send, 2)
    own_total = lax.dynamic_slice(total, (0, me * rows), (1, rows))
    target_adjoint = own_sum * (ratio / own_total).reshape(rows, 1)

    def cont(d, t, v, o):
        continuation_kernel(d, t, v, o, ratio=ratio)

    mine = call(cont, shape(sources, lanes), density, total, target_values, name="continuation")
    theirs = mine
    for shift in range(1, nt):
        moved = lax.ppermute(mine, "tgt", [(i, (i + shift) % nt) for i in range(nt)])
        theirs = moved if shift == 1 else theirs + moved
    source_value = call(value_kernel, shape(sources, lanes), mine, theirs, cash, salvage, switch_cost[None, :], name="value")
    return source_value, target_adjoint[None]


def solution(mesh):
    placed = (
        P(None, "src"),
        P(None, "tgt"),
        P(),
        P("tgt", None),
        P("src", None),
        P("src", None),
        P(),
        P("src", None),
        P("src", None),
    )
    return jax.shard_map(
        on_device,
        mesh=mesh,
        in_specs=placed,
        out_specs=(P("src", None), P("tgt", "src", None)),
        check_vma=False,
    )
```

```python
import math

import jax
import jax.numpy as jnp
from jax import lax
from jax.experimental import pallas as pl
from jax.experimental.pallas import tpu as pltpu
from jax.sharding import PartitionSpec as P


LOG2E = math.log2(math.e)
F32 = jnp.float32
BF16 = jnp.bfloat16
GRANT = 16 * 2**20


def split2(x):
    hi = x.astype(BF16)
    return hi, (x - hi.astype(F32)).astype(BF16)


def split3(x):
    hi = x.astype(BF16)
    rest = x - hi.astype(F32)
    mid = rest.astype(BF16)
    return hi, mid, (rest - mid.astype(F32)).astype(BF16)


def dot(left, right, left_dim, right_dim):
    return lax.dot_general(left, right, (((left_dim,), (right_dim,)), ((), ())), preferred_element_type=F32)


def source_terms(mean, scale):
    scaled = mean * scale
    offset = -0.5 * jnp.sum(scaled * mean, axis=0, keepdims=True)
    s1, s2, s3 = split3(scaled)
    row = lax.broadcasted_iota(jnp.int32, scaled.shape, 0)
    o1, o2, o3 = (jnp.broadcast_to(o.astype(F32), scaled.shape) for o in split3(offset))
    tail = jnp.where(row == 0, o1, jnp.where(row == 1, o2, jnp.where(row == 2, o3, 0.0))).astype(BF16)
    return jnp.concatenate([s1, s1, s2, s2, s1, s3, tail], axis=0)


def target_terms(points):
    t1, t2, t3 = split3(points)
    row = lax.broadcasted_iota(jnp.int32, points.shape, 0)
    tail = jnp.where(row < 3, 1.0, 0.0).astype(BF16)
    return jnp.concatenate([t1, t2, t1, t2, t3, t1, tail], axis=0)


def swap_pairs(x):
    lane = lax.broadcasted_iota(jnp.int32, x.shape, 1)
    width = x.shape[1]
    return jnp.where(lane % 2 == 0, pltpu.roll(x, width - 1, 1), pltpu.roll(x, 1, 1))


def column(row):
    n = row.shape[1]
    wide = jnp.broadcast_to(row, (n, n))
    diagonal = lax.broadcasted_iota(jnp.int32, (n, n), 0) == lax.broadcasted_iota(jnp.int32, (n, n), 1)
    return jnp.sum(jnp.where(diagonal, wide, 0.0), axis=1, keepdims=True)


def pack_kernel(mean, cotangent, decision, out):
    rows, lanes = cotangent.shape
    held = jnp.where(decision[...] == 0, cotangent[...], 0.0)
    moved = jnp.where(decision[...] == 1, cotangent[...], 0.0)
    out[0:rows, :] = held + swap_pairs(moved)
    factors = mean.shape[0]
    for part in range(mean.shape[1] // lanes):
        out[rows + part * factors : rows + (part + 1) * factors, :] = mean[:, part * lanes : (part + 1) * lanes]


def own_kernel(mean, precision, points, scale_out, terms_out, total_out):
    scale = column(precision[...]) * LOG2E
    scale_out[...] = jnp.broadcast_to(scale, scale_out.shape)
    left = source_terms(mean[...], scale)
    width = 256
    for j in range(points.shape[1] // width):
        cols = slice(j * width, (j + 1) * width)
        terms = target_terms(points[:, cols])
        terms_out[:, cols] = terms
        total_out[:, cols] = jnp.sum(jnp.exp2(dot(left, terms, 0, 0)), axis=0, keepdims=True)


def unpack_mean(block, factors):
    lanes = block.shape[1]
    body = block.shape[0] * lanes // (lanes + factors)
    return body, jnp.concatenate(
        [block[body + p * factors : body + (p + 1) * factors, :] for p in range(body // lanes)], axis=1
    )


def total_kernel(scale, terms, total, *refs):
    blocks, out = refs[:-1], refs[-1]
    lefts = [source_terms(unpack_mean(block, scale.shape[0])[1], scale[:, :1]) for block in blocks]
    width = 256
    for j in range(terms.shape[1] // width):
        cols = slice(j * width, (j + 1) * width)
        tile = sum(jnp.exp2(dot(left, terms[:, cols], 0, 0)) for left in lefts)
        out[:, cols] = total[:, cols] + jnp.sum(tile, axis=0, keepdims=True)


def continuation_kernel(mean, scale, terms, total, arrived, values, out, *, ratio):
    width = 256
    lanes = values.shape[1]
    left = source_terms(mean[...], scale[:, :1])
    acc = jnp.zeros((mean.shape[1], 2 * lanes), F32)
    low = jnp.zeros((mean.shape[1], lanes), F32)
    for j in range(terms.shape[1] // width):
        cols = slice(j * width, (j + 1) * width)
        factor = ratio / (total[:, cols] + arrived[:, cols])
        hi, lo = split2(jnp.exp2(dot(left, terms[:, cols], 0, 0)) * factor)
        vhi, vlo = split2(values[cols, :])
        acc += dot(hi, jnp.concatenate([vhi, vlo], axis=1), 1, 0)
        low += dot(lo, vhi, 1, 0)
    out[...] = acc[:, :lanes] + (acc[:, lanes:] + low)


def adjoint_kernel(where, scale, terms, *refs, masks):
    blocks, out = refs[:-1], refs[-1]
    lanes = out.shape[-1]
    rows = out.shape[1]
    rights, pairs = [], []
    for block in blocks:
        body, mean = unpack_mean(block, scale.shape[0])
        rights.append(source_terms(mean, scale[:, :1]))
        ahi, alo = split2(block[0:body, :])
        pairs.append((jnp.concatenate([ahi, alo], axis=1), ahi))
    for slot, mask in enumerate(masks):
        if rows % 128 == 0:
            start = pl.multiple_of((where[0] ^ mask) * rows, 128)
        else:
            start = slot * rows
        left = terms[:, pl.ds(start, rows)]
        acc = jnp.zeros((rows, 2 * lanes), F32)
        low = jnp.zeros((rows, lanes), F32)
        for right, (both, ahi) in zip(rights, pairs):
            hi, lo = split2(jnp.exp2(dot(left, right, 0, 0)))
            acc += dot(hi, both, 1, 0)
            low += dot(lo, ahi, 1, 0)
        out[slot] = acc[:, :lanes] + (acc[:, lanes:] + low)


def value_kernel(own, other, cash, salvage, cost, out):
    hold = own[...] + other[...] + cash[...]
    out[...] = jnp.maximum(jnp.maximum(hold, swap_pairs(hold) - cost[...]), salvage[...])


def finish_kernel(own, other, total, out, *, ratio):
    factor = column(ratio / total[...])
    out[...] = (own[...] + other[...]) * factor


def call(kernel, out_shape, *args):
    vmem = pl.BlockSpec(memory_space=pltpu.VMEM)
    smem = pl.BlockSpec(memory_space=pltpu.SMEM)
    specs, operands = [], []
    for a in args:
        if isinstance(a, Far):
            specs.append(vmem)
            operands.append(a.array)
        elif a.shape == (1,):
            specs.append(smem)
            operands.append(a)
        else:
            specs.append(vmem)
            operands.append(pltpu.with_memory_space_constraint(a, pltpu.VMEM))
    return pl.pallas_call(
        kernel,
        out_shape=out_shape,
        in_specs=specs,
        out_specs=jax.tree.map(lambda _: vmem, out_shape),
        compiler_params=pltpu.CompilerParams(vmem_limit_bytes=GRANT),
    )(*operands)


class Far:
    def __init__(self, array):
        self.array = array


def shape(*dims, dtype=F32):
    return pltpu.VMEM(dims, dtype)


def result(*dims):
    return jax.ShapeDtypeStruct(dims, F32)


def on_device(source_mean, target_points, precision, target_values, cash, salvage, switch_cost, cotangent, decision):
    n = lax.axis_size("src")
    nt = lax.axis_size("tgt")
    factors, sources = source_mean.shape
    targets = target_points.shape[1]
    lanes = cash.shape[1]
    me = lax.axis_index("src")
    where = me[None].astype(jnp.int32)
    ratio = (sources * n) / (targets * nt)
    rows = targets // n
    top = n // 2

    def flip(x, mask):
        return lax.ppermute(x, "src", [(i, i ^ mask) for i in range(n)])

    packed = call(
        pack_kernel, shape(sources + factors * sources // lanes, lanes), Far(source_mean), Far(cotangent), Far(decision)
    )
    groups = []
    blocks = [packed]
    bit, level = 2, 0
    while bit < top:
        span = min(4, top // bit)
        payload = blocks[0] if len(blocks) == 1 else jnp.stack(blocks)
        more = []
        for k in reversed(range(1, span)):
            r = flip(payload, k * bit)
            more.append([r] if len(blocks) == 1 else [r[b] for b in range(len(blocks))])
        if level == 0:
            groups += [[b for g in more[1:] for b in g], more[0]]
        else:
            groups += more
        blocks = blocks + [b for g in more for b in g]
        bit *= span
        level += 1

    scale, terms, total = call(
        own_kernel,
        (shape(factors, lanes), shape(7 * factors, targets, dtype=BF16), shape(1, targets)),
        Far(source_mean),
        Far(precision[None, :]),
        Far(target_points),
    )
    for group in groups:
        total = call(total_kernel, shape(1, targets), scale, terms, total, *group)
    total = total + flip(total, 1)
    arrived = flip(total, top)

    def adjoint(masks):
        if rows % 128 == 0:
            near = terms
        else:
            near = jnp.concatenate(
                [lax.dynamic_slice(terms, (0, (me ^ mask) * rows), (terms.shape[0], rows)) for mask in masks], axis=1
            )

        def kernel(*refs):
            adjoint_kernel(*refs, masks=masks)

        return call(kernel, shape(len(masks), rows, lanes), where, scale, near, *blocks)

    away = adjoint((1, 1 ^ top))
    came = flip(away, 1)
    near = adjoint((0, top))
    far_half = near[1] + came[1]
    came_far = flip(far_half, top)
    own_half = near[0] + came[0]
    own_total = lax.dynamic_slice(total, (0, me * rows), (1, rows)) + lax.dynamic_slice(arrived, (0, me * rows), (1, rows))

    def finish(a, b, t, o):
        finish_kernel(a, b, t, o, ratio=ratio)

    target_adjoint = call(finish, result(rows, lanes), own_half, came_far, own_total)

    def cont(*refs):
        continuation_kernel(*refs, ratio=ratio)

    mine = call(cont, shape(sources, lanes), source_mean, scale, terms, total, arrived, target_values)
    theirs = mine
    for shift in range(1, nt):
        moved = lax.ppermute(mine, "tgt", [(i, (i + shift) % nt) for i in range(nt)])
        theirs = moved if shift == 1 else theirs + moved
    source_value = call(value_kernel, result(sources, lanes), mine, theirs, cash, salvage, switch_cost[None, :])
    return source_value, target_adjoint[None]


def solution(mesh):
    placed = (
        P(None, "src"),
        P(None, "tgt"),
        P(),
        P("tgt", None),
        P("src", None),
        P("src", None),
        P(),
        P("src", None),
        P("src", None),
    )

    return jax.shard_map(
        on_device,
        mesh=mesh,
        in_specs=placed,
        out_specs=(P("src", None), P("tgt", "src", None)),
        check_vma=False,
    )
```

```python
import math

import jax
import jax.numpy as jnp
from jax import lax
from jax.experimental import pallas as pl
from jax.experimental.pallas import tpu as pltpu
from jax.sharding import PartitionSpec as P


LOG2E = math.log2(math.e)
F32 = jnp.float32
BF16 = jnp.bfloat16
GRANT = 16 * 2**20


def split2(x):
    hi = x.astype(BF16)
    return hi, (x - hi.astype(F32)).astype(BF16)


def split3(x):
    hi = x.astype(BF16)
    rest = x - hi.astype(F32)
    mid = rest.astype(BF16)
    return hi, mid, (rest - mid.astype(F32)).astype(BF16)


def dot(left, right, left_dim, right_dim):
    return lax.dot_general(left, right, (((left_dim,), (right_dim,)), ((), ())), preferred_element_type=F32)


def source_terms(mean, scale):
    scaled = mean * scale
    offset = -0.5 * jnp.sum(scaled * mean, axis=0, keepdims=True)
    s1, s2, s3 = split3(scaled)
    row = lax.broadcasted_iota(jnp.int32, scaled.shape, 0)
    o1, o2, o3 = (jnp.broadcast_to(o.astype(F32), scaled.shape) for o in split3(offset))
    tail = jnp.where(row == 0, o1, jnp.where(row == 1, o2, jnp.where(row == 2, o3, 0.0))).astype(BF16)
    return jnp.concatenate([s1, s1, s2, s2, s1, s3, tail], axis=0)


def target_terms(points):
    t1, t2, t3 = split3(points)
    row = lax.broadcasted_iota(jnp.int32, points.shape, 0)
    tail = jnp.where(row < 3, 1.0, 0.0).astype(BF16)
    return jnp.concatenate([t1, t2, t1, t2, t3, t1, tail], axis=0)


def swap_pairs(x):
    lane = lax.broadcasted_iota(jnp.int32, x.shape, 1)
    width = x.shape[1]
    return jnp.where(lane % 2 == 0, pltpu.roll(x, width - 1, 1), pltpu.roll(x, 1, 1))


def column(row):
    n = row.shape[1]
    wide = jnp.broadcast_to(row, (n, n))
    diagonal = lax.broadcasted_iota(jnp.int32, (n, n), 0) == lax.broadcasted_iota(jnp.int32, (n, n), 1)
    return jnp.sum(jnp.where(diagonal, wide, 0.0), axis=1, keepdims=True)


def load_kernel(cotangent, decision, mean, precision, points, adjoint_out, mean_out, precision_out, points_out, c, d, sems):
    pairs = ((cotangent, c), (decision, d), (points, points_out), (mean, mean_out), (precision, precision_out))
    copies = [pltpu.make_async_copy(src, dst, sems.at[i]) for i, (src, dst) in enumerate(pairs)]
    for copy in copies:
        copy.start()
    copies[0].wait()
    copies[1].wait()
    held = jnp.where(d[...] == 0, c[...], 0.0)
    moved = jnp.where(d[...] == 1, c[...], 0.0)
    adjoint_out[...] = held + swap_pairs(moved)
    for copy in copies[2:]:
        copy.wait()


def own_kernel(mean, precision, points, scale_out, terms_out, density_out, total_out):
    scale = column(precision[...]) * LOG2E
    scale_out[...] = jnp.broadcast_to(scale, scale_out.shape)
    left = source_terms(mean[...], scale)
    width = 256
    for j in range(points.shape[1] // width):
        cols = slice(j * width, (j + 1) * width)
        terms = target_terms(points[:, cols])
        terms_out[:, cols] = terms
        tile = jnp.exp2(dot(left, terms, 0, 0))
        density_out[:, cols] = tile
        total_out[:, cols] = jnp.sum(tile, axis=0, keepdims=True)


def total_kernel(scale, terms, total, *refs):
    means, out = refs[:-1], refs[-1]
    lefts = [source_terms(mean[...], scale[:, :1]) for mean in means]
    width = 256
    for j in range(terms.shape[1] // width):
        cols = slice(j * width, (j + 1) * width)
        tile = sum(jnp.exp2(dot(left, terms[:, cols], 0, 0)) for left in lefts)
        out[:, cols] = total[:, cols] + jnp.sum(tile, axis=0, keepdims=True)


def continuation_kernel(density, total, arrived, values, out, *, ratio):
    width = 256
    lanes = values.shape[1]
    acc = jnp.zeros((density.shape[0], 2 * lanes), F32)
    low = jnp.zeros((density.shape[0], lanes), F32)
    for j in range(density.shape[1] // width):
        cols = slice(j * width, (j + 1) * width)
        factor = ratio / (total[:, cols] + arrived[:, cols])
        hi, lo = split2(density[:, cols] * factor)
        vhi, vlo = split2(values[cols, :])
        acc += dot(hi, jnp.concatenate([vhi, vlo], axis=1), 1, 0)
        low += dot(lo, vhi, 1, 0)
    out[...] = acc[:, :lanes] + (acc[:, lanes:] + low)


def own_columns(mask, rows):
    return pl.multiple_of((lax.axis_index("src") ^ mask) * rows, 128) if rows % 128 == 0 else 0


def adjoint_kernel(scale, terms, *refs, mask):
    out = refs[-1]
    count = len(refs) // 2
    rows, lanes = out.shape
    left = terms[:, pl.ds(own_columns(mask, rows), rows)]
    acc = jnp.zeros((rows, 2 * lanes), F32)
    low = jnp.zeros((rows, lanes), F32)
    for mean, block in zip(refs[:count], refs[count:-1]):
        ahi, alo = split2(block[...])
        hi, lo = split2(jnp.exp2(dot(left, source_terms(mean[...], scale[:, :1]), 0, 0)))
        acc += dot(hi, jnp.concatenate([ahi, alo], axis=1), 1, 0)
        low += dot(lo, ahi, 1, 0)
    out[...] = acc[:, :lanes] + (acc[:, lanes:] + low)


def add_kernel(left, right, out):
    out[...] = left[...] + right[...]


def value_kernel(own, other, cash, salvage, cost, out):
    hold = own[...] + other[...] + cash[...]
    out[...] = jnp.maximum(jnp.maximum(hold, swap_pairs(hold) - cost[...]), salvage[...])


def finish_kernel(near, came, came_far, total, arrived, out, *, ratio):
    rows = out.shape[0]
    cols = pl.ds(own_columns(0, rows), rows)
    factor = column(ratio / (total[:, cols] + arrived[:, cols]))
    out[...] = (near[...] + came[...] + came_far[...]) * factor


def call(kernel, out_shape, *args, scratch=()):
    vmem = pl.BlockSpec(memory_space=pltpu.VMEM)
    specs, operands = [], []
    for a in args:
        if isinstance(a, Far):
            specs.append(pl.BlockSpec(memory_space=pltpu.HBM))
            operands.append(pltpu.with_memory_space_constraint(a.array, pltpu.HBM))
        else:
            specs.append(vmem)
            operands.append(pltpu.with_memory_space_constraint(a, pltpu.VMEM))
    return pl.pallas_call(
        kernel,
        out_shape=out_shape,
        in_specs=specs,
        out_specs=jax.tree.map(lambda _: vmem, out_shape),
        scratch_shapes=scratch,
        compiler_params=pltpu.CompilerParams(vmem_limit_bytes=GRANT),
    )(*operands)


class Far:
    def __init__(self, array):
        self.array = array


def shape(*dims, dtype=F32):
    return pltpu.VMEM(dims, dtype)


def result(*dims):
    return jax.ShapeDtypeStruct(dims, F32)


def on_device(source_mean, target_points, precision, target_values, cash, salvage, switch_cost, cotangent, decision):
    n = lax.axis_size("src")
    nt = lax.axis_size("tgt")
    factors, sources = source_mean.shape
    targets = target_points.shape[1]
    lanes = cash.shape[1]
    ratio = (sources * n) / (targets * nt)
    rows = targets // n
    top = n // 2

    def flip(x, mask):
        return lax.ppermute(x, "src", [(i, i ^ mask) for i in range(n)])

    def gather(x):
        blocks = [x]
        bit, level = 2, 0
        while bit < top:
            span = min(4, top // bit)
            payload = blocks[0] if len(blocks) == 1 else jnp.stack(blocks)
            more = [flip(payload, k * bit) for k in reversed(range(1, span))]
            more = [b for m in more for b in ([m] if len(blocks) == 1 else [m[i] for i in range(len(blocks))])]
            blocks = blocks + more
            bit *= span
            level += 1
        return blocks

    means = gather(source_mean)
    packed, mean, precision, points = call(
        load_kernel,
        (shape(sources, lanes), shape(factors, sources), shape(1, factors), shape(factors, targets)),
        Far(cotangent),
        Far(decision),
        Far(source_mean),
        Far(precision[None, :]),
        Far(target_points),
        scratch=(pltpu.VMEM((sources, lanes), F32), pltpu.VMEM((sources, lanes), jnp.int32), pltpu.SemaphoreType.DMA((5,))),
    )
    means[0] = mean
    packs = gather(packed)
    scale, terms, density, total = call(
        own_kernel,
        (shape(factors, lanes), shape(7 * factors, targets, dtype=BF16), shape(sources, targets), shape(1, targets)),
        mean,
        precision,
        points,
    )
    total = call(total_kernel, shape(1, targets), scale, terms, total, *means[1:])
    total = call(add_kernel, shape(1, targets), total, flip(total, 1))
    arrived = flip(total, top)

    def columns_of(x, mask):
        return x if rows % 128 == 0 else lax.dynamic_slice(x, (0, (lax.axis_index("src") ^ mask) * rows), (x.shape[0], rows))

    def adjoint(mask):
        def kernel(*refs):
            adjoint_kernel(*refs, mask=mask)

        return call(kernel, shape(rows, lanes), scale, columns_of(terms, mask), *means, *packs)

    came1 = flip(adjoint(1 ^ top), 1)
    far_half = call(add_kernel, shape(rows, lanes), adjoint(top), came1)
    came_far = flip(far_half, top)
    came0 = flip(adjoint(1), 1)
    near0 = adjoint(0)

    def finish(*refs):
        finish_kernel(*refs, ratio=ratio)

    target_adjoint = call(
        finish, result(rows, lanes), near0, came0, came_far, columns_of(total, 0), columns_of(arrived, 0)
    )

    def cont(*refs):
        continuation_kernel(*refs, ratio=ratio)

    mine = call(cont, shape(sources, lanes), density, total, arrived, target_values)
    theirs = mine
    for shift in range(1, nt):
        moved = lax.ppermute(mine, "tgt", [(i, (i + shift) % nt) for i in range(nt)])
        theirs = moved if shift == 1 else theirs + moved
    source_value = call(value_kernel, result(sources, lanes), mine, theirs, cash, salvage, switch_cost[None, :])
    return source_value, target_adjoint[None]


def solution(mesh):
    placed = (
        P(None, "src"),
        P(None, "tgt"),
        P(),
        P("tgt", None),
        P("src", None),
        P("src", None),
        P(),
        P("src", None),
        P("src", None),
    )

    return jax.shard_map(
        on_device,
        mesh=mesh,
        in_specs=placed,
        out_specs=(P("src", None), P("tgt", "src", None)),
        check_vma=False,
    )
```
